32 devices in a mesh: dp: 2 (over x), var: 4 (over y, core), mp: 4 (over z).
Axes of the slice: x: 2, y: 2, z: 4, core: 2. Of those that a mesh axis runs over, the one named last changes fastest.
Arguments:
- fields: bfloat16 [4, 48, 4, 512], P('dp', 'var'), may hold values from -6 to 6
- target: float32 [4, 512, 192], P('dp'), may hold values from -6 to 6
- lead_hours: int32 [4], P('dp'), may hold values from 6 to 168
- sources: int32 [4], replicated, may hold values from 0 to 4
- variables: int32 [48], P('var'), may hold values from 0 to 47, each once
- step_count: int32 [], replicated, may hold values from 2 to 20
- attention_weight: float32 [4, 1024, 1024], P(None, 'dp', ('var', 'mp')), may hold values from -0.1875 to 0.1875
- attention_moment: float32 [4, 1024, 1024], P(None, 'dp', ('var', 'mp')), may hold values from -1.9073486e-05 to 1.9073486e-05
- attention_square: float32 [4, 1024, 1024], P(None, 'dp', ('var', 'mp')), may hold values from 4.190733e-12 to 1.6665471e-11
- dense_weight: float32 [2, 1024, 4096], P(None, 'dp', ('var', 'mp')), may hold values from -0.1875 to 0.1875
- dense_moment: float32 [2, 1024, 4096], P(None, 'dp', ('var', 'mp')), may hold values from -1.9073486e-05 to 1.9073486e-05
- dense_square: float32 [2, 1024, 4096], P(None, 'dp', ('var', 'mp')), may hold values from 4.190733e-12 to 1.6665471e-11
- mixing_weight: float32 [3, 1024, 1024], P(None, ('dp', 'var'), 'mp'), may hold values from -0.1875 to 0.1875
- mixing_moment: float32 [3, 1024, 1024], P(None, ('dp', 'var'), 'mp'), may hold values from -1.9073486e-05 to 1.9073486e-05
- mixing_square: float32 [3, 1024, 1024], P(None, ('dp', 'var'), 'mp'), may hold values from 4.190733e-12 to 1.6665471e-11
- norm_gains: float32 [5, 1024], P(None, ('dp', 'var', 'mp')), may hold values from 0.5 to 1.5
- gains_moment: float32 [5, 1024], P(None, ('dp', 'var', 'mp')), may hold values from -7.6293945e-05 to 7.6293945e-05
- gains_square: float32 [5, 1024], P(None, ('dp', 'var', 'mp')), may hold values from 6.7051725e-11 to 2.6664754e-10
- position_table: float32 [512, 1024], P(None, ('dp', 'var', 'mp')), may hold values from -3 to 3
- position_moment: float32 [512, 1024], P(None, ('dp', 'var', 'mp')), may hold values from -5.9604645e-07 to 5.9604645e-07
- position_square: float32 [512, 1024], P(None, ('dp', 'var', 'mp')), may hold values from 4.2913103e-15 to 1.7065444e-14
- head_weight: float32 [192, 1024], P(None, ('dp', 'var', 'mp')), may hold values from -0.1875 to 0.1875
- head_moment: float32 [192, 1024], P(None, ('dp', 'var', 'mp')), may hold values from -7.6293945e-05 to 7.6293945e-05
- head_square: float32 [192, 1024], P(None, ('dp', 'var', 'mp')), may hold values from 6.7051725e-11 to 2.6664754e-10
- embed_table: float32 [240, 1024], P(None, ('dp', 'var', 'mp')), may hold values from -3 to 3
- embed_moment: float32 [240, 1024], P(None, ('dp', 'var', 'mp')), may hold values from -3.8146973e-06 to 3.8146973e-06
- embed_square: float32 [240, 1024], P(None, ('dp', 'var', 'mp')), may hold values from 1.6762931e-13 to 6.666189e-13
Outputs:
- loss_value: float32 [], replicated
- grad_norm: float32 [], replicated
- attention_new: float32 [4, 1024, 1024], P(None, 'dp', ('var', 'mp'))
- attention_moment_new: float32 [4, 1024, 1024], P(None, 'dp', ('var', 'mp'))
- attention_square_new: float32 [4, 1024, 1024], P(None, 'dp', ('var', 'mp'))
- dense_new: float32 [2, 1024, 4096], P(None, 'dp', ('var', 'mp'))
- dense_moment_new: float32 [2, 1024, 4096], P(None, 'dp', ('var', 'mp'))
- dense_square_new: float32 [2, 1024, 4096], P(None, 'dp', ('var', 'mp'))
- mixing_new: float32 [3, 1024, 1024], P(None, ('dp', 'var'), 'mp')
- mixing_moment_new: float32 [3, 1024, 1024], P(None, ('dp', 'var'), 'mp')
- mixing_square_new: float32 [3, 1024, 1024], P(None, ('dp', 'var'), 'mp')
- gains_new: float32 [5, 1024], P(None, ('dp', 'var', 'mp'))
- gains_moment_new: float32 [5, 1024], P(None, ('dp', 'var', 'mp'))
- gains_square_new: float32 [5, 1024], P(None, ('dp', 'var', 'mp'))
- position_new: float32 [512, 1024], P(None, ('dp', 'var', 'mp'))
- position_moment_new: float32 [512, 1024], P(None, ('dp', 'var', 'mp'))
- position_square_new: float32 [512, 1024], P(None, ('dp', 'var', 'mp'))
- head_new: float32 [192, 1024], P(None, ('dp', 'var', 'mp'))
- head_moment_new: float32 [192, 1024], P(None, ('dp', 'var', 'mp'))
- head_square_new: float32 [192, 1024], P(None, ('dp', 'var', 'mp'))
- embed_new: float32 [240, 1024], P(None, ('dp', 'var', 'mp'))
- embed_moment_new: float32 [240, 1024], P(None, ('dp', 'var', 'mp'))
- embed_square_new: float32 [240, 1024], P(None, ('dp', 'var', 'mp'))
- stream_rms: float32 [4], replicated
The draws below stay inside these ranges and needn't reach their ends.
Inputs may be any that keep to these rules, and one draw needn't show every extreme that they name: variables is a permutation of the 48 variables.
All inputs are finite; a program needn't handle non-finite values.
Results may differ from the reference program's by a relative error of at most 0.023.
Values may be sent and summed in bfloat16 or wider, within the bound.
A program may use at most 256 MiB of HBM per device.

```python
import math
import jax
import jax.numpy as jnp
from jax import lax

D = 1024
HEADS = 16
FF = 4096
VARS = 48
PIX = 4
PH = 16
PW = 32
NSRC = 5
P_SIZE = 512
C_OUT = 192
ITEMS = 4
NPAR = 16700416
N_VAR = 4
N_MP = 4


def set_ends(entries, own_key, smallest, high):
    longest = entries.shape.index(max(entries.shape))
    spots = []
    for shift in (0, 1):
        where = [jax.random.randint(jax.random.fold_in(own_key, axis), (), 0, length) for axis, length in enumerate(entries.shape)]
        where[longest] = (where[longest] + shift) % entries.shape[longest]
        spots.append(tuple(where))
    return entries.at[spots[0]].set(smallest).at[spots[1]].set(high)


def block_scale(stream_key, dims, cuts, least, top_value):
    def one(position, blocks):
        heights = jax.random.uniform(jax.random.fold_in(jax.random.fold_in(stream_key, 6), position), (blocks,), jnp.float32, least / len(cuts), top_value / len(cuts))
        return jnp.repeat(jnp.exp(heights), dims[position] // blocks).reshape((-1,) + (1,) * (len(dims) - position - 1))

    factor_of = one(*cuts[0])
    for cut in cuts[1:]:
        factor_of = factor_of * one(*cut)
    return factor_of


def scatter_about(own_key, shape, deviation, most, cuts=(), kind=jnp.bfloat16):
    values = jax.random.normal(own_key, shape, jnp.float32) * deviation
    if len(cuts) > 0:
        values = block_scale(own_key, shape, cuts, -0.22, 0.18) * values
    return jnp.clip(values, min=-most, max=most).astype(kind)


def setup_inputs(seed: int = 0) -> dict:
    arg_keys = jax.random.split(jax.random.key(seed), 28)
    fields = scatter_about(arg_keys[0], (ITEMS, VARS, PIX, P_SIZE), 1.0, 6.0, ((0, 2), (1, 4)))
    target = scatter_about(arg_keys[1], (ITEMS, P_SIZE, C_OUT), 1.0, 6.0, ((0, 2),), jnp.float32)
    lead_hours = set_ends(jax.random.randint(arg_keys[2], (ITEMS,), 6, 169), jax.random.fold_in(arg_keys[2], 1), 6, 168).astype(jnp.int32)
    sources = set_ends(jax.random.randint(arg_keys[3], (ITEMS,), 0, NSRC), jax.random.fold_in(arg_keys[3], 1), 0, NSRC - 1).astype(jnp.int32)
    variables = jax.random.permutation(arg_keys[4], VARS).astype(jnp.int32)
    step_count = jax.random.randint(arg_keys[5], (), 2, 21).astype(jnp.int32)
    attention_weight = scatter_about(arg_keys[6], (4, D, D), D ** -0.5, 0.1875, ((1, 2), (2, 16)), jnp.float32)
    attention_moment = scatter_about(arg_keys[7], (4, D, D), (0.25 * (D / (C_OUT * ITEMS * P_SIZE)) ** 0.5 / NPAR ** 0.5), 1.9073486328125e-05, ((1, 2), (2, 16)), jnp.float32)
    attention_square = jnp.clip(jnp.exp(math.log(1.6665471086474426e-11) - 1.3804634 * jax.random.uniform(arg_keys[8], (4, D, D), jnp.float32) ** block_scale(arg_keys[8], (4, D, D), ((1, 2), (2, 16)), -0.2, 0.2)), 4.190732830200439e-12, 1.6665471086474426e-11)
    dense_weight = scatter_about(arg_keys[9], (2, D, FF), D ** -0.5, 0.1875, ((1, 2), (2, 16)), jnp.float32)
    dense_moment = scatter_about(arg_keys[10], (2, D, FF), (0.25 * (D / (C_OUT * ITEMS * P_SIZE)) ** 0.5 / NPAR ** 0.5), 1.9073486328125e-05, ((1, 2), (2, 16)), jnp.float32)
    dense_square = jnp.clip(jnp.exp(math.log(1.6665471086474426e-11) - 1.3804634 * jax.random.uniform(arg_keys[11], (2, D, FF), jnp.float32) ** block_scale(arg_keys[11], (2, D, FF), ((1, 2), (2, 16)), -0.2, 0.2)), 4.190732830200439e-12, 1.6665471086474426e-11)
    mixing_weight = scatter_about(arg_keys[12], (3, D, D), D ** -0.5, 0.1875, ((1, 8), (2, 4)), jnp.float32)
    mixing_moment = scatter_about(arg_keys[13], (3, D, D), (0.25 * (D / (C_OUT * ITEMS * P_SIZE)) ** 0.5 / NPAR ** 0.5), 1.9073486328125e-05, ((1, 8), (2, 4)), jnp.float32)
    mixing_square = jnp.clip(jnp.exp(math.log(1.6665471086474426e-11) - 1.3804634 * jax.random.uniform(arg_keys[14], (3, D, D), jnp.float32) ** block_scale(arg_keys[14], (3, D, D), ((1, 8), (2, 4)), -0.2, 0.2)), 4.190732830200439e-12, 1.6665471086474426e-11)
    norm_gains = jnp.clip(1.0 + 0.1 * jax.random.normal(arg_keys[15], (5, D), jnp.float32), 0.5, 1.5)
    gains_moment = scatter_about(arg_keys[16], (5, D), (1.0 * (D / (C_OUT * ITEMS * P_SIZE)) ** 0.5 / NPAR ** 0.5), 7.62939453125e-05, ((1, 32),), jnp.float32)
    gains_square = jnp.clip(jnp.exp(math.log(2.666475373835908e-10) - 1.3804634 * jax.random.uniform(arg_keys[17], (5, D), jnp.float32) ** block_scale(arg_keys[17], (5, D), ((1, 32),), -0.2, 0.2)), 6.705172528320702e-11, 2.666475373835908e-10)
    position_table = scatter_about(arg_keys[18], (P_SIZE, D), 0.5, 3.0, ((1, 32),), jnp.float32)
    position_moment = scatter_about(arg_keys[19], (P_SIZE, D), (0.008 * (D / (C_OUT * ITEMS * P_SIZE)) ** 0.5 / NPAR ** 0.5), 5.960464477539062e-07, ((1, 32),), jnp.float32)
    position_square = jnp.clip(jnp.exp(math.log(1.706544383887551e-14) - 1.3804635 * jax.random.uniform(arg_keys[20], (P_SIZE, D), jnp.float32) ** block_scale(arg_keys[20], (P_SIZE, D), ((1, 32),), -0.2, 0.2)), 4.291310315180253e-15, 1.706544383887551e-14)
    head_weight = scatter_about(arg_keys[21], (C_OUT, D), D ** -0.5, 0.1875, ((1, 32),), jnp.float32)
    head_moment = scatter_about(arg_keys[22], (C_OUT, D), (1.0 * (D / (C_OUT * ITEMS * P_SIZE)) ** 0.5 / NPAR ** 0.5), 7.62939453125e-05, ((1, 32),), jnp.float32)
    head_square = jnp.clip(jnp.exp(math.log(2.666475373835908e-10) - 1.3804634 * jax.random.uniform(arg_keys[23], (C_OUT, D), jnp.float32) ** block_scale(arg_keys[23], (C_OUT, D), ((1, 32),), -0.2, 0.2)), 6.705172528320702e-11, 2.666475373835908e-10)
    embed_table = scatter_about(arg_keys[24], (VARS * (PIX + 1), D), 0.5, 3.0, ((1, 32),), jnp.float32)
    embed_moment = scatter_about(arg_keys[25], (VARS * (PIX + 1), D), (0.05 * (D / (C_OUT * ITEMS * P_SIZE)) ** 0.5 / NPAR ** 0.5), 3.814697265625e-06, ((1, 32),), jnp.float32)
    embed_square = jnp.clip(jnp.exp(math.log(6.666188868270639e-13) - 1.38046344 * jax.random.uniform(arg_keys[26], (VARS * (PIX + 1), D), jnp.float32) ** block_scale(arg_keys[26], (VARS * (PIX + 1), D), ((1, 32),), -0.2, 0.2)), 1.676293110396132e-13, 6.666188868270639e-13)
    return {"fields": fields, "target": target, "lead_hours": lead_hours, "sources": sources, "variables": variables, "step_count": step_count, "attention_weight": attention_weight, "attention_moment": attention_moment, "attention_square": attention_square, "dense_weight": dense_weight, "dense_moment": dense_moment, "dense_square": dense_square, "mixing_weight": mixing_weight, "mixing_moment": mixing_moment, "mixing_square": mixing_square, "norm_gains": norm_gains, "gains_moment": gains_moment, "gains_square": gains_square, "position_table": position_table, "position_moment": position_moment, "position_square": position_square, "head_weight": head_weight, "head_moment": head_moment, "head_square": head_square, "embed_table": embed_table, "embed_moment": embed_moment, "embed_square": embed_square}


HIGHEST = lax.Precision.HIGHEST
NORM_EPS = 1e-05
BETA_ONE = 0.5
BETA_TWO = 0.7
ADAM_EPS = 1e-08
DECAY = 0.01

@jax.custom_vjp
def low(v):
    return lax.optimization_barrier(v.astype(jnp.bfloat16)).astype(jnp.float32)

@jax.custom_vjp
def low_back(v):
    return v

def low_keep(v):
    return (low(v), None)

def low_pass(kept, grad):
    return (grad,)

def back_keep(v):
    return (v, None)

def back_low(kept, grad):
    return (low(grad),)
low.defvjp(low_keep, low_pass)
low_back.defvjp(back_keep, back_low)

def layer_norm(values, gain_row):
    centred = values - lax.optimization_barrier(jnp.mean(values, -1, keepdims=True))
    return centred * lax.rsqrt(lax.optimization_barrier(jnp.mean(centred * centred, -1, keepdims=True)) + NORM_EPS) * gain_row

def latitude_weights():
    angles = (jnp.arange(PH, dtype=jnp.float32) + 0.5) * (math.pi / PH) - math.pi / 2
    cosine = jnp.cos(angles)
    return jnp.repeat(cosine / jnp.mean(cosine), PW)

def group_sum(left_rows, right_cols, groups):
    row_count, inner_width = left_rows.shape
    parts = jnp.einsum('pgk,dgk->gpd', left_rows.reshape(row_count, groups, inner_width // groups), right_cols.reshape(right_cols.shape[0], groups, inner_width // groups), precision=HIGHEST)
    return low_back(lax.optimization_barrier(jnp.sum(low(parts), 0)))

def item_loss(params, item_data, variables):
    attention_weight, dense_weight, mixing_weight, norm_gains, position_table, head_weight, embed_table = params
    field_item, target_item, lead_item, scale_item = item_data
    head_dim = D // HEADS
    groups = N_VAR * N_MP
    slot_table = embed_table.reshape(VARS, PIX + 1, D)[variables]
    field_ones = jnp.concatenate([field_item, jnp.ones((VARS, 1, P_SIZE), jnp.float32)], 1)
    embeds = low(jnp.einsum('vcp,vcd->vpd', field_ones, slot_table, precision=HIGHEST))
    key_matrix = low(mixing_weight[0])
    value_matrix = low(mixing_weight[1])
    out_matrix = low(mixing_weight[2])
    key_query = low(jnp.einsum('dhk,hk->dh', key_matrix.reshape(D, HEADS, head_dim), norm_gains[4].reshape(HEADS, head_dim), precision=HIGHEST))
    variable_scores = low_back(jnp.einsum('vpd,dh->vph', embeds, key_query, precision=HIGHEST) / math.sqrt(head_dim))
    variable_values = low_back(low(jnp.einsum('vpd,de->vpe', embeds, value_matrix, precision=HIGHEST)))
    mix_weights = jax.nn.softmax(variable_scores, axis=0)
    mixed_rows = low(jnp.einsum('vph,vphk->phk', mix_weights, variable_values.reshape(VARS, P_SIZE, HEADS, head_dim), precision=HIGHEST).reshape(P_SIZE, D))
    start_rows = group_sum(mixed_rows, out_matrix, N_MP)
    residual0 = start_rows + position_table + lead_item * norm_gains[3]
    normed1 = low(layer_norm(residual0, norm_gains[0]))
    projected = low_back(low(jnp.einsum('pd,sde->spe', normed1, low(attention_weight[:3]), precision=HIGHEST)))
    heads_view = projected.reshape(3, P_SIZE, HEADS, head_dim)
    scores = low_back(jnp.einsum('qhk,thk->hqt', heads_view[0], heads_view[1], precision=HIGHEST) / math.sqrt(head_dim))
    soft_weights = low(jax.nn.softmax(scores, axis=-1))
    attended = low_back(low(jnp.einsum('hqt,thk->qhk', soft_weights, heads_view[2], precision=HIGHEST).reshape(P_SIZE, D)))
    attend_out = group_sum(attended, low(attention_weight[3]), groups)
    residual1 = residual0 + attend_out
    normed2 = low(layer_norm(residual1, norm_gains[1]))
    pre_act = low_back(jnp.dot(normed2, low(dense_weight[0]), precision=HIGHEST))
    activated = low(jax.nn.gelu(pre_act, approximate=False))
    dense_out = group_sum(activated, low(dense_weight[1]), groups)
    residual2 = residual1 + dense_out
    normed3 = low(layer_norm(residual2, norm_gains[2]))
    predicted = jnp.dot(normed3, low(head_weight).T, precision=HIGHEST)
    errors = predicted - target_item
    item_total = scale_item * jnp.sum(latitude_weights()[:, None] * errors * errors)
    stats = jnp.stack([jnp.sum(start_rows * start_rows), jnp.sum(attend_out * attend_out), jnp.sum(dense_out * dense_out), jnp.sum(residual2 * residual2)])
    return (item_total, stats)

def adam_update(weight, gradient, first_moment, second, factor, step_value, step_rate, decay_rate):
    clipped = gradient * factor
    first_moment = BETA_ONE * first_moment + (1.0 - BETA_ONE) * clipped
    second = BETA_TWO * second + (1.0 - BETA_TWO) * clipped * clipped
    normalized = first_moment / (1.0 - jnp.power(BETA_ONE, step_value)) / (jnp.sqrt(second / (1.0 - jnp.power(BETA_TWO, step_value))) + ADAM_EPS)
    return (weight - step_rate * (normalized + decay_rate * weight), first_moment, second)

def reference(fields, target, lead_hours, sources, variables, step_count, attention_weight, attention_moment, attention_square, dense_weight, dense_moment, dense_square, mixing_weight, mixing_moment, mixing_square, norm_gains, gains_moment, gains_square, position_table, position_moment, position_square, head_weight, head_moment, head_square, embed_table, embed_moment, embed_square):
    weights = (attention_weight, dense_weight, mixing_weight, norm_gains, position_table, head_weight, embed_table)
    moments = (attention_moment, dense_moment, mixing_moment, gains_moment, position_moment, head_moment, embed_moment)
    squares = (attention_square, dense_square, mixing_square, gains_square, position_square, head_square, embed_square)
    counts = lax.optimization_barrier(jnp.sum((sources[:, None] == jnp.arange(NSRC)[None, :]).astype(jnp.float32), 0))
    scales = 1.0 / (NSRC * P_SIZE * PIX * VARS * counts[sources])
    inputs = (fields.astype(jnp.float32), target, lead_hours.astype(jnp.float32) / 100.0, scales)

    def total_loss(params):

        def step_item(carry, item_data):
            item_total, stats = jax.checkpoint(item_loss)(params, item_data, variables)
            return ((carry[0] + item_total, carry[1] + stats), None)
        start = (jnp.zeros((), jnp.float32), jnp.zeros((4,), jnp.float32))
        (total, stats), _ = lax.scan(step_item, start, inputs)
        return (total, stats)
    loss_value, pullback, stats = jax.vjp(total_loss, weights, has_aux=True)
    grads = pullback(jnp.ones((), jnp.float32))[0]
    grad_norm = jnp.sqrt(sum((jnp.sum(gradient * gradient) for gradient in grads)))
    clip_at = 0.25 * math.sqrt(D / (VARS * PIX * ITEMS * P_SIZE))
    factor = jnp.minimum(1.0, clip_at / grad_norm)
    step_value = step_count.astype(jnp.float32)
    matrix_rate = 0.5 / math.sqrt(D)
    rates = (matrix_rate, matrix_rate, matrix_rate, 0.2, 0.2, matrix_rate, 0.2)
    decays = (DECAY, DECAY, DECAY, 0.0, DECAY, DECAY, DECAY)
    updated = []
    for index in range(7):
        updated.extend(adam_update(weights[index], grads[index], moments[index], squares[index], factor, step_value, rates[index], decays[index]))
    stream_rms = jnp.sqrt(stats / (ITEMS * P_SIZE * D))
    return (loss_value, grad_norm, updated[0], updated[1], updated[2], updated[3], updated[4], updated[5], updated[6], updated[7], updated[8], updated[9], updated[10], updated[11], updated[12], updated[13], updated[14], updated[15], updated[16], updated[17], updated[18], updated[19], updated[20], stream_rms)
```

```python
import math
import types

import jax
import jax.numpy as jnp
from jax import lax
from jax.experimental import pallas as pl
from jax.experimental.pallas import tpu as pltpu
from jax.sharding import PartitionSpec as P

D = 1024
HEADS = 16
VARS = 48
PIX = 4
PH = 16
PW = 32
NSRC = 5
P_SIZE = 512
C_OUT = PIX * VARS
HEAD_DIM = D // HEADS
TERMS = VARS * (PIX + 1)

HIGHEST = lax.Precision.HIGHEST
FLOAT = jnp.float32
BFLOAT = jnp.bfloat16
NORM_EPS = 1e-05
BETA_ONE = 0.5
BETA_TWO = 0.7
ADAM_EPS = 1e-08
DECAY = 0.01
MESH = pl.DeviceIdType.MESH

ROWS = 64
HALF = ROWS // 2
PAIR = 2 * ROWS
PAD = 16
ROOT = math.sqrt(HEAD_DIM)


def place():
    x, w, z = lax.axis_index("dp"), lax.axis_index("var"), lax.axis_index("mp")
    y, c, group, low = lax.div(w, 2), lax.rem(w, 2), lax.div(z, 2), lax.rem(z, 2)
    return types.SimpleNamespace(
        x=x, w=w, z=z, y=y, c=c, group=group, low=low,
        core_peer={"var": 2 * y + (1 - c)},
        y_peer={"var": 2 * (1 - y) + c},
        z_peer={"mp": 2 * group + (1 - low)},
        pair_peer={"mp": 2 * (1 - group) + low},
    )


def sizes():
    dp, var, mp = lax.axis_size("dp"), lax.axis_size("var"), lax.axis_size("mp")
    return types.SimpleNamespace(dp=dp, var=var, mp=mp, plane=dp * var, all=dp * var * mp)


def device_of(index):
    n = sizes()
    return {
        "dp": lax.div(index, n.var * n.mp),
        "var": lax.rem(lax.div(index, n.mp), n.var),
        "mp": lax.rem(index, n.mp),
    }


class Links:
    def __init__(self, send, recv):
        self.send, self.recv, self.used = send, recv, 0
        self.open = []

    def start(self, src, dst, device):
        index = self.used
        self.used += 1
        copy = pltpu.make_async_remote_copy(
            src_ref=src, dst_ref=dst, send_sem=self.send.at[index], recv_sem=self.recv.at[index],
            device_id=device, device_id_type=MESH,
        )
        copy.start()
        self.open.append(copy)
        return copy

    def finish_sends(self):
        for copy in self.open:
            copy.wait_send()
        self.open = []


def wait_all(copies):
    for copy in copies:
        copy.wait_recv()


def at_rows(index, size, unit=None):
    return pl.ds(pl.multiple_of(index * size, unit or size), size)


def wide(value):
    return value.astype(FLOAT)


def dot(a, b, dims=((1,), (0,)), precision=None):
    return lax.dot_general(a, b, (dims, ((), ())), precision=precision, preferred_element_type=FLOAT)


ROWS_ROWS = ((0,), (0,))
COLS_COLS = ((1,), (1,))


def center(values):
    centred = values - jnp.mean(values, -1, keepdims=True)
    inverse = lax.rsqrt(jnp.mean(centred * centred, -1, keepdims=True) + NORM_EPS)
    return centred * inverse, inverse


def norm_backward(grad_out, unit_rows, inverse, gain_row):
    scaled = grad_out * gain_row
    return inverse * (
        scaled
        - jnp.mean(scaled, -1, keepdims=True)
        - unit_rows * jnp.mean(scaled * unit_rows, -1, keepdims=True)
    )


def column_sum(values):
    return jnp.sum(values, 0, keepdims=True)


def gelu(values):
    return 0.5 * values * (1.0 + lax.erf(values * (1.0 / math.sqrt(2.0))))


def gelu_slope(values):
    bell = jnp.exp(-0.5 * values * values) * (1.0 / math.sqrt(2.0 * math.pi))
    return 0.5 * (1.0 + lax.erf(values * (1.0 / math.sqrt(2.0)))) + values * bell


def square_sum(links, p, part, buffers, fill, during=None):
    core_in, held, diag_in, diag_out, last_in = buffers
    sides = (1 - p.y, p.y)
    first = []
    for k, side in enumerate(sides):
        theirs = 2 * side + (1 - p.c)
        fill(theirs)
        first.append(links.start(part.at[at_rows(theirs, PAIR)], core_in.at[k], p.core_peer))
    for side in sides:
        fill(2 * side + p.c)
    for k, side in enumerate(sides):
        first[k].wait_recv()
        held[k] = (wide(part[at_rows(2 * side + p.c, PAIR), :]) + wide(core_in[k])).astype(BFLOAT)

    def piece(which, offset):
        return pl.ds(pl.multiple_of(which * ROWS + offset, HALF), HALF)

    top, end = pl.ds(0, HALF), pl.ds(HALF, HALF)
    diag_z = links.start(held.at[0, piece(1 - p.low, 0)], diag_in.at[0], p.z_peer)
    diag_y = links.start(held.at[0, piece(1 - p.low, HALF)], diag_in.at[1], p.y_peer)
    last = [
        links.start(held.at[0, piece(p.low, HALF)], last_in.at[0, end], p.y_peer),
        links.start(held.at[1, piece(1 - p.low, 0)], last_in.at[1, top], p.z_peer),
    ]
    diag_z.wait_recv()
    diag_out[0] = (wide(held[0, piece(p.low, 0), :]) + wide(diag_in[0])).astype(BFLOAT)
    last.append(links.start(diag_out.at[0], last_in.at[0, top], p.y_peer))
    diag_y.wait_recv()
    diag_out[1] = (wide(held[1, piece(1 - p.low, HALF), :]) + wide(diag_in[1])).astype(BFLOAT)
    last.append(links.start(diag_out.at[1], last_in.at[1, end], p.z_peer))
    if during is not None:
        during()
    wait_all(last)
    return wide(held[1, at_rows(p.low, ROWS), :]) + wide(last_in[0]) + wide(last_in[1])


def square_gather(links, p, out, own_rows, during=None):
    def rows(y, low, offset=0, size=ROWS):
        return out.at[pl.ds(pl.multiple_of((4 * y + 2 * p.c + low) * ROWS + offset, HALF), size)]

    own, from_y, from_z = rows(p.y, p.low), rows(1 - p.y, p.low), rows(p.y, 1 - p.low)
    own[...] = own_rows.astype(BFLOAT)
    y_top, z_end = rows(1 - p.y, p.low, 0, HALF), rows(p.y, 1 - p.low, HALF, HALF)
    far_top, far_end = rows(1 - p.y, 1 - p.low, 0, HALF), rows(1 - p.y, 1 - p.low, HALF, HALF)
    to_y = links.start(own, own, p.y_peer)
    to_z = links.start(own, own, p.z_peer)
    last = [links.start(own, own, p.core_peer)]
    if during is not None:
        during()
    to_y.wait_recv()
    y_to_z = links.start(y_top, y_top, p.z_peer)
    last.append(links.start(from_y, from_y, p.core_peer))
    to_z.wait_recv()
    z_to_y = links.start(z_end, z_end, p.y_peer)
    last.append(links.start(from_z, from_z, p.core_peer))
    y_to_z.wait_recv()
    last.append(links.start(far_top, far_top, p.core_peer))
    z_to_y.wait_recv()
    last.append(links.start(far_end, far_end, p.core_peer))
    wait_all(last)


def plane_sum(links, p, part, total, parts_in, dp_in, held):
    n = sizes()
    rows = part.shape[0] // n.var
    copies = []
    for k in range(1, n.var):
        other = lax.rem(p.w + k, n.var)
        copies.append(links.start(part.at[at_rows(other, rows)], parts_in.at[k - 1], {"var": other}))
    mine = part[at_rows(p.w, rows), :]
    for k, copy in enumerate(copies):
        copy.wait_recv()
        mine = mine + parts_in[k]
    held[...] = mine
    copies = [links.start(held, dp_in.at[k - 1], {"dp": lax.rem(p.x + k, n.dp)}) for k in range(1, n.dp)]
    for k, copy in enumerate(copies):
        copy.wait_recv()
        mine = mine + dp_in[k]
    total[at_rows(p.w, rows), :] = mine
    own = total.at[at_rows(p.w, rows)]
    wait_all([links.start(own, own, {"var": lax.rem(p.w + k, n.var)}) for k in range(1, n.var)])


def stack_rows(target, pieces, count, rows, kind):
    if rows % (16 if kind == BFLOAT else 8) == 0:
        target[...] = pieces[...].reshape(count * rows, pieces.shape[-1]).astype(target.dtype)
    else:
        for k in range(count):
            target[k * rows : (k + 1) * rows, :] = pieces[k].astype(target.dtype)


def step_shapes():
    n = sizes()
    columns = D // n.all
    split = D // n.dp
    plane_rows = D // n.plane
    mix = D // n.mp
    mix_rows = 2 * PAIR
    slots = PAD * n.var
    vmem = pltpu.VMEM
    inputs = [
        "lead_hours", "sources", "latitude", "fields", "target", "attention", "dense", "mixing", "gains", "pos",
        "head", "emb",
    ]
    outs = dict(
        g_attention=((4, HEAD_DIM, split), FLOAT),
        g_dense=((2, split, 256), FLOAT),
        g_mixing=((3, plane_rows, mix), FLOAT),
        g_gains=((5, columns), FLOAT),
        g_pos=((columns, P_SIZE), FLOAT),
        g_head=((columns, C_OUT), FLOAT),
        g_emb=((columns, TERMS), FLOAT),
        totals=((8, 128), FLOAT),
    )
    b, f = BFLOAT, FLOAT
    scratch = dict(
        att=vmem((2, n.dp, 4 * HEAD_DIM, split), b),
        ffw=vmem((2, 2, D, 256), b),
        emb_all=vmem((n.mp, columns, TERMS), f),
        emb_rows=vmem((n.mp * columns, TERMS), f),
        fields_all=vmem((n.var, PIX + 1, PAD, mix_rows), b),
        gains_all=vmem((n.all, 5, columns), f),
        gain_rows=vmem((8, D), f),
        head_own=vmem((columns, C_OUT), b),
        head_all=vmem((n.all, columns, C_OUT), b),
        head_rows=vmem((D, C_OUT), b),
        pos_own=vmem((columns, P_SIZE), b),
        pos_all=vmem((n.all, columns, PAIR), b),
        pos_cols=vmem((D, PAIR), f),
        pos_rows=vmem((PAIR, D), f),
        own_out=vmem((plane_rows, mix), b),
        out_all=vmem((n.plane, plane_rows, mix), b),
        out_rows=vmem((D, mix), b),
        key_query=vmem((plane_rows, 128), f),
        tables_part=vmem((256, mix), f),
        tables=vmem((256, mix), f),
        tables_in=vmem((n.var - 1, 256 // n.var, mix), f),
        tables_dp=vmem((n.dp - 1, 256 // n.var, mix), f),
        tables_held=vmem((256 // n.var, mix), f),
        sides_part=vmem((256, mix), f),
        sides=vmem((256, mix), f),
        sides_in=vmem((n.var - 1, 256 // n.var, mix), f),
        sides_dp=vmem((n.dp - 1, 256 // n.var, mix), f),
        sides_held=vmem((256 // n.var, mix), f),
        pick=vmem(((PIX + 1) * slots, TERMS), f),
        slot_table=vmem(((PIX + 1) * slots, mix), f),
        terms=vmem((PIX, slots, mix_rows), f),
        mix_weights=vmem((mix // HEAD_DIM, slots, mix_rows), f),
        mixed=vmem((mix_rows, mix), b),
        start_part=vmem((mix_rows, D), b),
        start_in=vmem((n.mp - 1, ROWS, D), b),
        start_grad=vmem((mix_rows, D), b),
        part0=vmem((P_SIZE, D), b),
        part1=vmem((P_SIZE, D), b),
        part2=vmem((P_SIZE, D), b),
        part3=vmem((P_SIZE, D), b),
        n1=vmem((P_SIZE, D), b),
        n2=vmem((P_SIZE, D), b),
        g2=vmem((P_SIZE, D), b),
        g1=vmem((P_SIZE, D), b),
        res0=vmem((ROWS, D), f),
        res1=vmem((ROWS, D), f),
        gres=vmem((ROWS, D), f),
        n3=vmem((ROWS, D), b),
        grad_pred=vmem((ROWS, C_OUT), f),
        proj=vmem((2, P_SIZE, 3 * HEAD_DIM), b),
        gproj=vmem((2, P_SIZE, 3 * HEAD_DIM), b),
        weights=vmem((2, P_SIZE, P_SIZE), f),
        dscores=vmem((2, P_SIZE, P_SIZE), b),
        attended=vmem((P_SIZE, 2 * HEAD_DIM), b),
        gattended=vmem((P_SIZE, 2 * HEAD_DIM), b),
        pre=vmem((P_SIZE, 512), f),
        act=vmem((P_SIZE, 512), b),
        gpre=vmem((P_SIZE, 512), b),
        target_own=vmem((ROWS, C_OUT), f),
        ga=vmem((n.dp, 2, 4 * HEAD_DIM, split), b),
        ga_in=vmem((n.dp - 1, 2, 4 * HEAD_DIM, split), b),
        ga_pair=vmem((4 * HEAD_DIM, split), b),
        ga_pair_in=vmem((4 * HEAD_DIM, split), b),
        ga_mine=vmem((4 * HEAD_DIM, split), f),
        gd=vmem((n.dp, 2, 2, split, 256), b),
        gd_in=vmem((n.dp - 1, 2, 2, split, 256), b),
        gd_pair=vmem((2, split, 256), b),
        gd_pair_in=vmem((2, split, 256), b),
        gd_mine=vmem((2, split, 256), f),
        gh=vmem((n.all, columns, C_OUT), b),
        gh_in=vmem((n.all, columns, C_OUT), b),
        gp=vmem((n.all, columns, PAIR), f),
        gp_in=vmem((n.plane, columns, PAIR), f),
        gp_sum=vmem((columns, PAIR), f),
        gp_all=vmem((n.var, columns, PAIR), f),
        ge=vmem((n.mp, columns, TERMS), f),
        ge_in=vmem((n.mp, columns, TERMS), f),
        gw=vmem((n.plane, plane_rows, mix), b),
        gw_in=vmem((n.plane, plane_rows, mix), b),
        gg=vmem((8, D), f),
        gg_in=vmem((n.all, 8, 128), f),
        tile=vmem((8, 128), f),
        tiles=vmem((n.all, 8, 128), f),
    )
    for k in range(4):
        scratch.update(
            {
                f"core_in{k}": vmem((2, PAIR, D), b),
                f"held{k}": vmem((2, PAIR, D), b),
                f"diag_in{k}": vmem((2, HALF, D), b),
                f"diag_out{k}": vmem((2, HALF, D), b),
                f"last_in{k}": vmem((2, ROWS, D), b),
            }
        )
    count = 160 + 12 * n.dp
    scratch.update(
        send=pltpu.SemaphoreType.DMA((count,)),
        recv=pltpu.SemaphoreType.DMA((count,)),
        send_all=pltpu.SemaphoreType.DMA((4, n.all)),
        recv_all=pltpu.SemaphoreType.DMA((4, n.all)),
        send_plane=pltpu.SemaphoreType.DMA((3, n.plane)),
        recv_plane=pltpu.SemaphoreType.DMA((3, n.plane)),
        local=pltpu.SemaphoreType.DMA((1,)),
    )
    return inputs, outs, scratch


def step_kernel(names, *refs):
    r = types.SimpleNamespace(**dict(zip(names, refs)))
    n, p = sizes(), place()
    x, w, z = p.x, p.w, p.z
    me, plane_me = (x * n.var + w) * n.mp + z, x * n.var + w
    columns, split, plane_rows, mix = D // n.all, D // n.dp, D // n.plane, D // n.mp
    mix_heads, slots = mix // HEAD_DIM, PAD * n.var
    local_vars = VARS // n.var
    links = Links(r.send, r.recv)

    def buffers(k):
        return [getattr(r, f"{name}{k}") for name in ("core_in", "held", "diag_in", "diag_out", "last_in")]

    def everyone(kind, count, make):
        send, recv = (r.send_all, r.recv_all) if count == n.all else (r.send_plane, r.recv_plane)

        def copy(k):
            src, dst, device = make(k)
            return pltpu.make_async_remote_copy(
                src_ref=src, dst_ref=dst, send_sem=send.at[kind, k], recv_sem=recv.at[kind, k],
                device_id=device, device_id_type=MESH,
            )

        def run(action):
            def one(k, _):
                action(copy(k))
                return 0

            lax.fori_loop(1, count, one, 0)

        return run

    def begin(copy):
        copy.start()

    def arrive(copy):
        copy.wait_recv()

    def leave(copy):
        copy.wait_send()

    barrier = pltpu.get_barrier_semaphore()

    def signal(k, _):
        pl.semaphore_signal(
            barrier, inc=1, device_id=device_of(lax.rem(me + k, n.all)), device_id_type=MESH
        )
        return 0

    lax.fori_loop(1, n.all, signal, 0)
    own_target = pltpu.make_async_copy(
        r.target.at[p.group, at_rows(2 * w + p.low, ROWS), :], r.target_own, r.local.at[0]
    )
    own_target.start()
    r.att[p.group, x] = r.attention[...].reshape(4 * HEAD_DIM, split).astype(BFLOAT)
    own_split = at_rows(x, split)
    for k in range(2):
        r.ffw[p.group, k, own_split, :] = r.dense[k].astype(BFLOAT)
    r.own_out[...] = r.mixing[2].astype(BFLOAT)
    r.out_all[plane_me] = r.mixing[2].astype(BFLOAT)
    r.head_own[...] = r.head[...].astype(BFLOAT)
    r.head_all[me] = r.head[...].astype(BFLOAT)
    r.pos_own[...] = r.pos[...].astype(BFLOAT)
    r.pos_all[me] = r.pos[:, at_rows(w, PAIR)].astype(BFLOAT)
    r.emb_all[z] = r.emb[...]
    r.fields_all[w] = r.fields[w]
    r.gains_all[me] = r.gains[...]
    pl.semaphore_wait(barrier, n.all - 1)

    emb_copies = [
        links.start(r.emb, r.emb_all.at[z], {"mp": lax.rem(z + k, n.mp)}) for k in range(1, n.mp)
    ]

    def to_device(k):
        other = lax.rem(me + k, n.all)
        return other, device_of(other)

    def to_plane(k):
        other = lax.rem(plane_me + k, n.plane)
        return other, {"dp": lax.div(other, n.var), "var": lax.rem(other, n.var)}

    gains_run = everyone(0, n.all, lambda k: (r.gains, r.gains_all.at[me], to_device(k)[1]))
    gains_run(begin)
    field_copies = []
    for k in range(1, n.var):
        other = lax.rem(w + k, n.var)
        field_copies.append(links.start(r.fields.at[other], r.fields_all.at[w], {"var": other}))
    att_pair = links.start(r.att.at[p.group, x], r.att.at[p.group, x], p.pair_peer)
    out_run = everyone(0, n.plane, lambda k: (r.own_out, r.out_all.at[plane_me], to_plane(k)[1]))
    out_run(begin)

    def pos_make(k):
        device = to_device(k)[1]
        return r.pos_own.at[:, at_rows(device["var"], PAIR)], r.pos_all.at[me], device

    pos_run = everyone(1, n.all, pos_make)
    pos_run(begin)

    key_own, value_own = wide(r.mixing[0].astype(BFLOAT)), wide(r.mixing[1].astype(BFLOAT))
    wait_all(emb_copies)
    stack_rows(r.emb_rows, r.emb_all, n.mp, columns, FLOAT)
    emb_rows = r.emb_rows[...]
    r.tables_part[0:TERMS, :] = dot(emb_rows, value_own, ROWS_ROWS, HIGHEST)
    gains_run(arrive)
    for k in range(n.all):
        r.gain_rows[0:5, k * columns : (k + 1) * columns] = r.gains_all[k]
    query = r.gain_rows[4:5, at_rows(z, mix)]
    head_of = (
        lax.div(lax.broadcasted_iota(jnp.int32, (mix, 128), 0), HEAD_DIM)
        == lax.broadcasted_iota(jnp.int32, (mix, 128), 1)
    ).astype(FLOAT)
    r.key_query[...] = wide(dot(key_own * query, head_of, precision=HIGHEST).astype(BFLOAT))
    r.tables_part[TERMS:256, :] = jnp.zeros((256 - TERMS, mix), FLOAT)
    score_part = dot(r.key_query[...], emb_rows, ROWS_ROWS, HIGHEST)
    r.tables_part[TERMS : TERMS + 8, 0:TERMS] = score_part[0:8, :]
    plane_sum(links, p, r.tables_part, r.tables, r.tables_in, r.tables_dp, r.tables_held)

    def to_dp(copies, src, dst):
        for k in range(1, n.dp):
            copies.append(links.start(src, dst, {"dp": lax.rem(x + k, n.dp)}))

    att_copies, dense_copies = [], []
    to_dp(att_copies, r.att.at[p.group, x], r.att.at[p.group, x])

    wait_all(field_copies)
    every = r.fields_all[...]
    ids = wide(every[:, PIX, :, 0:1]).reshape(slots, 1)
    term_index = lax.broadcasted_iota(jnp.int32, (slots, TERMS), 1).astype(FLOAT)
    for c in range(PIX + 1):
        r.pick[c * slots : (c + 1) * slots, :] = (term_index == ids * (PIX + 1.0) + c).astype(FLOAT)
    r.slot_table[...] = dot(r.pick[...], r.tables[0:TERMS, :], precision=HIGHEST)
    slot_scores = dot(r.pick[...], r.tables[TERMS : TERMS + 8, 0:TERMS], COLS_COLS, HIGHEST)
    for c in range(PIX):
        r.terms[c] = wide(every[:, c]).reshape(slots, 2 * PAIR)
    used = lax.rem(lax.broadcasted_iota(jnp.int32, (slots, 1), 0), PAD) < local_vars
    terms = [r.terms[c] for c in range(PIX)]
    mixed = []

    def stacked(weights):
        return jnp.concatenate([term * weights for term in terms] + [weights], 0)

    for h in range(mix_heads):
        scores = slot_scores[PIX * slots :, h : h + 1]
        for c in range(PIX):
            scores = scores + terms[c] * slot_scores[c * slots : (c + 1) * slots, h : h + 1]
        scores = jnp.where(used, scores * (1.0 / ROOT), -1e30)
        shifted = jnp.exp(scores - jnp.max(scores, 0, keepdims=True))
        weights = shifted / jnp.sum(shifted, 0, keepdims=True)
        r.mix_weights[h] = weights
        mixed.append(
            dot(stacked(weights), r.slot_table[:, h * HEAD_DIM : (h + 1) * HEAD_DIM], ROWS_ROWS, HIGHEST)
        )
    r.mixed[...] = jnp.concatenate(mixed, 1).astype(BFLOAT)
    out_run(arrive)
    stack_rows(r.out_rows, r.out_all, n.plane, plane_rows, BFLOAT)
    r.start_part[...] = dot(r.mixed[...], r.out_rows[...], COLS_COLS).astype(BFLOAT)
    start_copies = []
    for k in range(1, n.mp):
        other = lax.rem(z + k, n.mp)
        start_copies.append(
            links.start(r.start_part.at[at_rows(other, ROWS)], r.start_in.at[k - 1], {"mp": other})
        )
    to_dp(dense_copies, r.ffw.at[p.group, :, own_split], r.ffw.at[p.group, :, own_split])
    att_pair.wait_recv()
    to_dp(att_copies, r.att.at[1 - p.group, x], r.att.at[1 - p.group, x])
    pos_run(arrive)
    stack_rows(r.pos_cols, r.pos_all, n.all, columns, BFLOAT)
    r.pos_rows[...] = r.pos_cols[...].T
    lead = r.lead_hours[p.group].astype(FLOAT) / 100.0
    start = wide(r.start_part[at_rows(z, ROWS), :])
    for k, copy in enumerate(start_copies):
        copy.wait_recv()
        start = start + wide(r.start_in[k])
    start_square = column_sum(start * start)
    residual = start + r.pos_rows[at_rows(p.low, ROWS), :] + lead * r.gain_rows[3:4, :]
    r.res0[...] = residual
    unit, _ = center(residual)
    dense_pair = [links.start(r.ffw.at[p.group, 0, own_split], r.ffw.at[p.group, 0, own_split], p.pair_peer)]
    square_gather(links, p, r.n1, unit * r.gain_rows[0:1, :])
    dense_pair.append(
        links.start(r.ffw.at[p.group, 1, own_split], r.ffw.at[p.group, 1, own_split], p.pair_peer)
    )
    head_run = everyone(2, n.all, lambda k: (r.head_own, r.head_all.at[me], to_device(k)[1]))
    head_run(begin)

    wait_all(att_copies)
    qkv = 3 * HEAD_DIM
    for s in range(2):
        total = dot(r.n1[:, 0:split], r.att[s, 0, 0:qkv, :], COLS_COLS)
        for k in range(1, n.dp):
            total = total + dot(r.n1[:, k * split : (k + 1) * split], r.att[s, k, 0:qkv, :], COLS_COLS)
        r.proj[s] = total.astype(BFLOAT)

    def head_cols(s, which):
        return r.proj[s, :, which * HEAD_DIM : (which + 1) * HEAD_DIM]

    def attention_rows(index):
        rows = at_rows(index, PAIR)
        for s in range(2):
            queries = r.proj[s, rows, 0:HEAD_DIM]
            scores = dot(queries, head_cols(s, 1), COLS_COLS) * (1.0 / ROOT)
            shifted = jnp.exp(scores - jnp.max(scores, -1, keepdims=True))
            weights = shifted / jnp.sum(shifted, -1, keepdims=True)
            r.weights[s, rows, :] = weights
            r.attended[rows, s * HEAD_DIM : (s + 1) * HEAD_DIM] = dot(
                weights.astype(BFLOAT), head_cols(s, 2)
            ).astype(BFLOAT)
        for k in range(n.dp):
            both = jnp.concatenate([r.att[0, k, qkv:, :], r.att[1, k, qkv:, :]], 0)
            r.part0[rows, k * split : (k + 1) * split] = dot(r.attended[rows, :], both).astype(BFLOAT)

    attend = square_sum(links, p, r.part0, buffers(0), attention_rows)
    attend_square = column_sum(attend * attend)
    residual = r.res0[...] + attend
    r.res1[...] = residual
    unit, _ = center(residual)
    wait_all(dense_pair)
    for k in range(2):
        to_dp(dense_copies, r.ffw.at[1 - p.group, k, own_split], r.ffw.at[1 - p.group, k, own_split])
    square_gather(links, p, r.n2, unit * r.gain_rows[1:2, :])

    wait_all(dense_copies)
    hidden = [slice(s * 256, (s + 1) * 256) for s in range(2)]

    def forward_rows(index):
        rows = at_rows(index, PAIR)
        total = None
        for s in range(2):
            pre = dot(r.n2[rows, :], r.ffw[s, 0])
            r.pre[rows, hidden[s]] = pre
            act = gelu(pre).astype(BFLOAT)
            r.act[rows, hidden[s]] = act
            down = dot(act, r.ffw[s, 1], COLS_COLS)
            total = down if total is None else total + down
        r.part1[rows, :] = total.astype(BFLOAT)

    dense = square_sum(links, p, r.part1, buffers(1), forward_rows)
    dense_square = column_sum(dense * dense)
    residual = r.res1[...] + dense
    last_square = column_sum(residual * residual)
    unit, inverse = center(residual)
    head_run(arrive)
    stack_rows(r.head_rows, r.head_all, n.all, columns, BFLOAT)
    normed = (unit * r.gain_rows[2:3, :]).astype(BFLOAT)
    r.n3[...] = normed
    own_source = r.sources[x * 2 + p.group]
    count = jnp.float32(0.0)
    for k in range(r.sources.shape[0]):
        count = count + jnp.where(r.sources[k] == own_source, 1.0, 0.0)
    scale = 1.0 / (NSRC * P_SIZE * C_OUT * count)
    block = 2 * w + p.low
    first_half = lax.broadcasted_iota(jnp.int32, (ROWS, 1), 0) < PW
    row_weight = jnp.where(first_half, r.latitude[2 * block], r.latitude[2 * block + 1]) * scale
    own_target.wait()
    errors = dot(normed, r.head_rows[...]) - r.target_own[...]
    weighted = row_weight * errors
    loss_row = column_sum(weighted * errors)
    grad_pred = 2.0 * weighted
    r.grad_pred[...] = grad_pred
    grad_normed = dot(grad_pred, wide(r.head_rows[...]), COLS_COLS, HIGHEST)
    r.gg[2:3, :] = column_sum(grad_normed * unit)
    grad = norm_backward(grad_normed, unit, inverse, r.gain_rows[2:3, :])
    r.gres[...] = grad

    def head_grads():
        grad_head = dot(wide(r.n3[...]), r.grad_pred[...], ROWS_ROWS, HIGHEST).astype(BFLOAT)
        if columns % 16 == 0:
            r.gh[...] = grad_head.reshape(n.all, columns, C_OUT)
        else:
            for k in range(n.all):
                r.gh[k] = grad_head[k * columns : (k + 1) * columns]

    square_gather(links, p, r.g2, grad, head_grads)
    r.gh_in[me] = r.gh[me]

    def gh_make(k):
        other, device = to_device(k)
        return r.gh.at[other], r.gh_in.at[me], device

    gh_run = everyone(3, n.all, gh_make)
    gh_run(begin)

    def backward_rows(index):
        rows = at_rows(index, PAIR)
        total = None
        for s in range(2):
            grad_act = dot(r.g2[rows, :], r.ffw[s, 1])
            grad_pre = (grad_act * gelu_slope(r.pre[rows, hidden[s]])).astype(BFLOAT)
            r.gpre[rows, hidden[s]] = grad_pre
            back = dot(grad_pre, r.ffw[s, 0], COLS_COLS)
            total = back if total is None else total + back
        r.part2[rows, :] = total.astype(BFLOAT)

    def dense_grads(which):
        for s in range(2):
            if which == 1:
                grad = dot(r.g2[...], r.act[:, hidden[s]], ROWS_ROWS)
            else:
                grad = dot(r.n2[...], r.gpre[:, hidden[s]], ROWS_ROWS)
            for k in range(n.dp):
                r.gd[k, s, which] = grad[k * split : (k + 1) * split].astype(BFLOAT)

    grad_normed = square_sum(links, p, r.part2, buffers(2), backward_rows, lambda: dense_grads(1))
    unit, inverse = center(r.res1[...])
    r.gg[1:2, :] = column_sum(grad_normed * unit)
    grad = r.gres[...] + norm_backward(grad_normed, unit, inverse, r.gain_rows[1:2, :])
    r.gres[...] = grad
    square_gather(links, p, r.g1, grad, lambda: dense_grads(0))

    def over_dp(src, dst):
        return [
            links.start(src.at[lax.rem(x + k, n.dp)], dst.at[k - 1], {"dp": lax.rem(x + k, n.dp)})
            for k in range(1, n.dp)
        ]

    gd_copies = over_dp(r.gd, r.gd_in)

    for s in range(2):
        total = dot(r.g1[:, 0:split], r.att[s, 0, qkv:, :], COLS_COLS)
        for k in range(1, n.dp):
            total = total + dot(r.g1[:, k * split : (k + 1) * split], r.att[s, k, qkv:, :], COLS_COLS)
        r.gattended[:, s * HEAD_DIM : (s + 1) * HEAD_DIM] = total.astype(BFLOAT)

    def score_rows(index, _):
        rows = at_rows(index, PAIR)
        for s in range(2):
            grad_att = r.gattended[rows, s * HEAD_DIM : (s + 1) * HEAD_DIM]
            change = dot(grad_att, head_cols(s, 2), COLS_COLS)
            weights = r.weights[s, rows, :]
            grad_scores = (
                weights * (change - jnp.sum(weights * change, -1, keepdims=True))
            ).astype(BFLOAT)
            r.dscores[s, rows, :] = grad_scores
            r.gproj[s, rows, 0:HEAD_DIM] = (dot(grad_scores, head_cols(s, 1)) * (1.0 / ROOT)).astype(BFLOAT)
        return 0

    lax.fori_loop(0, P_SIZE // PAIR, score_rows, 0)
    for s in range(2):
        r.gproj[s, :, HEAD_DIM : 2 * HEAD_DIM] = (
            dot(r.dscores[s], head_cols(s, 0), ROWS_ROWS) * (1.0 / ROOT)
        ).astype(BFLOAT)
        r.gproj[s, :, 2 * HEAD_DIM :] = dot(
            r.weights[s].astype(BFLOAT), r.gattended[:, s * HEAD_DIM : (s + 1) * HEAD_DIM], ROWS_ROWS
        ).astype(BFLOAT)

    wait_all(gd_copies)

    def summed(own, incoming, s):
        total = wide(own[s])
        for k in range(n.dp - 1):
            total = total + wide(incoming[k, s])
        return total

    gd_own = r.gd.at[x]
    r.gd_mine[...] = summed(gd_own, r.gd_in, p.group)
    r.gd_pair[...] = summed(gd_own, r.gd_in, 1 - p.group).astype(BFLOAT)
    gd_pair = links.start(r.gd_pair, r.gd_pair_in, p.pair_peer)

    def entry_rows(index):
        rows = at_rows(index, PAIR)
        for k in range(n.dp):
            total = dot(r.gproj[0, rows, :], r.att[0, k, 0:qkv, :]) + dot(
                r.gproj[1, rows, :], r.att[1, k, 0:qkv, :]
            )
            r.part3[rows, k * split : (k + 1) * split] = total.astype(BFLOAT)

    def attention_grads():
        for s in range(2):
            grad = dot(r.gproj[s], r.n1[...], ROWS_ROWS)
            for k in range(n.dp):
                r.ga[k, s, 0:qkv, :] = grad[:, k * split : (k + 1) * split].astype(BFLOAT)
        grad = dot(r.attended[...], r.g1[...], ROWS_ROWS)
        for s in range(2):
            for k in range(n.dp):
                r.ga[k, s, qkv:, :] = grad[
                    s * HEAD_DIM : (s + 1) * HEAD_DIM, k * split : (k + 1) * split
                ].astype(BFLOAT)

    grad_normed = square_sum(links, p, r.part3, buffers(3), entry_rows, attention_grads)
    unit, inverse = center(r.res0[...])
    r.gg[0:1, :] = column_sum(grad_normed * unit)
    grad = r.gres[...] + norm_backward(grad_normed, unit, inverse, r.gain_rows[0:1, :])
    r.gg[3:4, :] = lead * column_sum(grad)
    own_rows = r.start_grad.at[at_rows(z, ROWS)]
    own_rows[...] = grad.astype(BFLOAT)
    grad_copies = [
        links.start(own_rows, own_rows, {"mp": lax.rem(z + k, n.mp)}) for k in range(1, n.mp)
    ]
    ga_copies = over_dp(r.ga, r.ga_in)
    wait_all(grad_copies)

    grads = r.start_grad[...]
    grad_mixed = dot(grads, r.out_rows[...])
    for h in range(mix_heads):
        cols = slice(h * HEAD_DIM, (h + 1) * HEAD_DIM)
        weights = r.mix_weights[h]
        through = dot(r.slot_table[:, cols], grad_mixed[:, cols], COLS_COLS, HIGHEST)
        change = through[PIX * slots :]
        for c in range(PIX):
            change = change + terms_of(r, c) * through[c * slots : (c + 1) * slots]
        grad_scores = weights * (change - jnp.sum(weights * change, 0, keepdims=True))
        stack = jnp.concatenate([terms_of(r, c) * weights for c in range(PIX)] + [weights], 0)
        r.side_slots[:, cols] = dot(stack, grad_mixed[:, cols], precision=HIGHEST)
        for c in range(PIX + 1):
            value = terms_of(r, c) * grad_scores if c < PIX else grad_scores
            r.score_slots[c * slots : (c + 1) * slots, h : h + 1] = jnp.sum(value, 1, keepdims=True) * (
                1.0 / ROOT
            )
    r.sides_part[0:TERMS, :] = dot(r.pick[...], r.side_slots[...], ROWS_ROWS, HIGHEST)
    r.sides_part[TERMS:256, :] = jnp.zeros((256 - TERMS, mix), FLOAT)
    r.sides_part[TERMS : TERMS + 8, 0:TERMS] = dot(r.score_slots[...], r.pick[...], ROWS_ROWS, HIGHEST)[0:8, :]
    items = wide(grads[0:PAIR, :]) + wide(grads[PAIR:, :])
    by_column = items.T
    if columns % 8 == 0:
        r.gp[...] = by_column.reshape(n.all, columns, PAIR)
    else:
        for k in range(n.all):
            r.gp[k] = by_column[k * columns : (k + 1) * columns]

    def gp_make(k):
        other, device = to_plane(k)
        return r.gp.at[other * n.mp + z], r.gp_in.at[plane_me], device

    r.gp_in[plane_me] = r.gp[me]
    plane_sum(links, p, r.sides_part, r.sides, r.sides_in, r.sides_dp, r.sides_held)
    gp_run = everyone(1, n.plane, gp_make)
    gp_run(begin)
    grad_out = dot(grads, r.mixed[...], ROWS_ROWS).astype(BFLOAT)
    r.gw[...] = grad_out.reshape(n.plane, plane_rows, mix)
    r.gw_in[plane_me] = r.gw[plane_me]

    def gw_make(k):
        other, device = to_plane(k)
        return r.gw.at[other], r.gw_in.at[plane_me], device

    gw_run = everyone(2, n.plane, gw_make)
    gw_run(begin)

    value_total = r.sides[0:TERMS, :]
    score_total = r.sides[TERMS : TERMS + 8, 0:TERMS]
    emb_rows = r.emb_rows[...]
    query = r.gain_rows[4:5, at_rows(z, mix)]
    grad_emb = dot(wide(r.mixing[1].astype(BFLOAT)), value_total, COLS_COLS, HIGHEST) + dot(
        r.key_query[:, 0:8], score_total, precision=HIGHEST
    )
    if columns % 8 == 0:
        r.ge[...] = grad_emb.reshape(n.mp, columns, TERMS)
    else:
        for k in range(n.mp):
            r.ge[k] = grad_emb[k * columns : (k + 1) * columns]
    r.ge_in[z] = r.ge[z]
    emb_copies = []
    for k in range(1, n.mp):
        other = lax.rem(z + k, n.mp)
        emb_copies.append(links.start(r.ge.at[other], r.ge_in.at[z], {"mp": other}))
    grad_kq = dot(emb_rows, score_total, COLS_COLS, HIGHEST)
    spread = jnp.concatenate(
        [jnp.broadcast_to(grad_kq[:, h : h + 1], (plane_rows, HEAD_DIM)) for h in range(mix_heads)], 1
    )
    r.gg[4:5, :] = jnp.zeros((1, D), FLOAT)
    r.gg[4:5, at_rows(z, mix)] = column_sum(wide(r.mixing[0].astype(BFLOAT)) * spread)
    r.gg[5:8, :] = jnp.zeros((3, D), FLOAT)
    lane_group = lax.div(me * columns, 128)

    def gg_make(k):
        other, device = to_device(k)
        return r.gg.at[:, at_rows(lax.div(other * columns, 128), 128)], r.gg_in.at[me], device

    gains_run(leave)
    gg_run = everyone(0, n.all, gg_make)
    gg_run(begin)
    r.gg_in[me] = r.gg[:, at_rows(lane_group, 128)]
    r.g_mixing[0] = spread * query
    r.g_mixing[1] = dot(emb_rows, value_total, precision=HIGHEST)

    wait_all(ga_copies)
    ga_own = r.ga.at[x]
    r.ga_mine[...] = summed(ga_own, r.ga_in, p.group)
    r.ga_pair[...] = summed(ga_own, r.ga_in, 1 - p.group).astype(BFLOAT)
    ga_pair = links.start(r.ga_pair, r.ga_pair_in, p.pair_peer)

    gp_run(arrive)
    r.gp_sum[...] = jnp.zeros((columns, PAIR), FLOAT)
    for v in range(n.var):
        total = r.gp_in[v]
        for k in range(1, n.dp):
            total = total + r.gp_in[k * n.var + v]
        r.g_pos[:, v * PAIR : (v + 1) * PAIR] = total
    gd_pair.wait_recv()
    r.g_dense[...] = r.gd_mine[...] + wide(r.gd_pair_in[...])
    gh_run(arrive)
    r.g_head[...] = lax.fori_loop(
        0, n.all, lambda k, so_far: so_far + wide(r.gh_in[k]), jnp.zeros((columns, C_OUT), FLOAT)
    )
    gw_run(arrive)
    r.g_mixing[2] = lax.fori_loop(
        0, n.plane, lambda k, so_far: so_far + wide(r.gw_in[k]), jnp.zeros((plane_rows, mix), FLOAT)
    )
    wait_all(emb_copies)
    grad_emb = r.ge_in[0]
    for k in range(1, n.mp):
        grad_emb = grad_emb + r.ge_in[k]
    r.g_emb[...] = grad_emb
    gg_run(arrive)
    gains_sum = lax.fori_loop(
        0, n.all, lambda k, so_far: so_far + r.gg_in[k], jnp.zeros((8, 128), FLOAT)
    )
    lane = lax.broadcasted_iota(jnp.int32, (128, columns), 0)
    offset = me * columns - lane_group * 128
    choose = (lane == lax.broadcasted_iota(jnp.int32, (128, columns), 1) + offset).astype(FLOAT)
    r.g_gains[...] = dot(gains_sum, choose, precision=HIGHEST)[0:5, :]
    ga_pair.wait_recv()
    r.g_attention[...] = (r.ga_mine[...] + wide(r.ga_pair_in[...])).reshape(4, HEAD_DIM, split)

    def square(ref):
        return jnp.sum(ref[...] * ref[...])

    squares = sum(
        square(ref)
        for ref in (r.g_attention, r.g_dense, r.g_mixing, r.g_gains, r.g_pos, r.g_head, r.g_emb)
    )
    line = lax.broadcasted_iota(jnp.int32, (8, 128), 0)
    tile = jnp.zeros((8, 128), FLOAT)
    for k, value in enumerate(
        (
            squares, jnp.sum(loss_row), jnp.sum(start_square), jnp.sum(attend_square), jnp.sum(dense_square),
            jnp.sum(last_square),
        )
    ):
        tile = jnp.where(line == k, value, tile)
    r.tile[...] = tile
    r.tiles[me] = tile
    pos_run(leave)
    tile_run = everyone(1, n.all, lambda k: (r.tile, r.tiles.at[me], to_device(k)[1]))
    tile_run(begin)
    for run in (out_run, head_run, gh_run, gp_run, gw_run, gg_run):
        run(leave)
    links.finish_sends()
    tile_run(arrive)
    r.totals[...] = lax.fori_loop(
        0, n.all, lambda k, so_far: so_far + r.tiles[k], jnp.zeros((8, 128), FLOAT)
    )
    tile_run(leave)


def terms_of(r, c):
    return r.terms[c]


def run_step(values):
    inputs, outs, scratch = step_shapes()
    n = sizes()
    mix = D // n.mp
    scratch["side_slots"] = pltpu.VMEM(((PIX + 1) * PAD * n.var, mix), FLOAT)
    scratch["score_slots"] = pltpu.VMEM(((PIX + 1) * PAD * n.var, 128), FLOAT)
    names = inputs + list(outs) + list(scratch)
    spaces = {"lead_hours": pltpu.SMEM, "sources": pltpu.SMEM, "latitude": pltpu.SMEM, "target": pl.ANY}

    def kernel(*refs):
        step_kernel(names, *refs)

    results = pl.pallas_call(
        kernel,
        out_shape=[jax.ShapeDtypeStruct(shape, kind) for shape, kind in outs.values()],
        in_specs=[pl.BlockSpec(memory_space=spaces.get(name, pltpu.VMEM)) for name in inputs],
        out_specs=[pl.BlockSpec(memory_space=pltpu.VMEM)] * len(outs),
        scratch_shapes=list(scratch.values()),
        compiler_params=pltpu.CompilerParams(
            collective_id=0, has_side_effects=True, vmem_limit_bytes=58000 * 1024
        ),
        name="step",
    )(*[values[name] for name in inputs])
    return dict(zip(outs, results))


RATES = (0.5 / math.sqrt(D), 0.5 / math.sqrt(D), 0.5 / math.sqrt(D), 0.2, 0.2, 0.5 / math.sqrt(D), 0.2)
DECAYS = (DECAY, DECAY, DECAY, 0.0, DECAY, DECAY, DECAY)


def update_kernel(items_all, step_count, totals, *refs):
    clip_at = 0.25 * math.sqrt(D / (VARS * PIX * items_all * P_SIZE))
    norm = jnp.sqrt(totals[0:1, 0:1])
    factor = jnp.minimum(1.0, clip_at / norm)
    step_value = jnp.zeros((1, 1), FLOAT) + step_count[0].astype(FLOAT)
    first_scale = 1.0 / (1.0 - jnp.exp(step_value * math.log(BETA_ONE)))
    second_scale = 1.0 / (1.0 - jnp.exp(step_value * math.log(BETA_TWO)))
    loss_out, norm_out, rms_out = refs[28 + 21 :]
    loss_out[...] = totals[1:2, 0:1]
    norm_out[...] = norm
    rms_out[...] = jnp.sqrt(totals[...] * (1.0 / (items_all * P_SIZE * D)))
    for index in range(7):
        weight, first, second, grad = refs[4 * index : 4 * index + 4]
        weight_out, first_out, second_out = refs[28 + 3 * index : 31 + 3 * index]

        def one(w, m, v, g, index=index):
            clipped = g * factor
            m = BETA_ONE * m + (1.0 - BETA_ONE) * clipped
            v = BETA_TWO * v + (1.0 - BETA_TWO) * clipped * clipped
            normalized = m * first_scale / (jnp.sqrt(v * second_scale) + ADAM_EPS)
            return w - RATES[index] * (normalized + DECAYS[index] * w), m, v

        results = one(weight[...], first[...], second[...], grad[...])
        for out, value in zip((weight_out, first_out, second_out), results):
            out[...] = value


def run_update(items_all, step_count, totals, groups):
    arrays = [array for group in groups for array in group]
    outs = [jax.ShapeDtypeStruct(group[0].shape, FLOAT) for group in groups for _ in range(3)]
    outs += [jax.ShapeDtypeStruct((1, 1), FLOAT)] * 2 + [jax.ShapeDtypeStruct((8, 128), FLOAT)]

    def kernel(*refs):
        update_kernel(items_all, *refs)

    return pl.pallas_call(
        kernel,
        out_shape=outs,
        in_specs=[pl.BlockSpec(memory_space=pltpu.SMEM)]
        + [pl.BlockSpec(memory_space=pltpu.VMEM)] * (1 + len(arrays)),
        out_specs=[pl.BlockSpec(memory_space=pltpu.VMEM)] * len(outs),
        compiler_params=pltpu.CompilerParams(vmem_limit_bytes=40000 * 1024),
        name="update",
    )(step_count.reshape(1), totals, *arrays)


def body(
    fields, target, lead_hours, sources, variables, step_count,
    attention_weight, attention_moment, attention_square,
    dense_weight, dense_moment, dense_square,
    mixing_weight, mixing_moment, mixing_square,
    norm_gains, gains_moment, gains_square,
    position_table, position_moment, position_square,
    head_weight, head_moment, head_square,
    embed_table, embed_moment, embed_square,
):
    n = sizes()
    local_items, local_vars = fields.shape[0], fields.shape[1]
    items_all = sources.shape[0]
    angles = (jnp.arange(PH, dtype=FLOAT) + 0.5) * (math.pi / PH) - math.pi / 2
    cosine = jnp.cos(angles)
    mix_rows = 2 * PAIR
    ids = jnp.broadcast_to(variables.astype(BFLOAT)[None, :, None], (1, local_vars, mix_rows))
    send = []
    for v in range(n.var):
        piece = fields[:, :, :, v * PAIR : (v + 1) * PAIR].transpose(2, 1, 0, 3)
        send.append(jnp.concatenate([piece.reshape(PIX, local_vars, mix_rows), ids], 0))
    send = jnp.pad(
        jnp.stack(send), ((0, 0), (0, 0), (0, PAD - local_vars), (0, 0))
    )
    blank = jnp.arange(PAD) >= local_vars
    plane = jnp.arange(PIX + 1) == PIX
    send = jnp.where(
        (blank[None, :] & plane[:, None])[None, :, :, None], jnp.asarray(-100.0, BFLOAT), send
    )

    def turned(array):
        return jnp.swapaxes(array, -1, -2)

    grads = run_step(
        dict(
            lead_hours=lead_hours, sources=sources, latitude=cosine / jnp.mean(cosine), fields=send,
            target=target, attention=turned(attention_weight), dense=dense_weight, mixing=mixing_weight,
            gains=norm_gains, pos=turned(position_table), head=turned(head_weight), emb=turned(embed_table),
        )
    )
    same = lambda array: array
    plan = (
        (turned, attention_weight, attention_moment, attention_square, grads["g_attention"]),
        (same, dense_weight, dense_moment, dense_square, grads["g_dense"]),
        (same, mixing_weight, mixing_moment, mixing_square, grads["g_mixing"]),
        (same, norm_gains, gains_moment, gains_square, grads["g_gains"]),
        (turned, position_table, position_moment, position_square, grads["g_pos"]),
        (turned, head_weight, head_moment, head_square, grads["g_head"]),
        (turned, embed_table, embed_moment, embed_square, grads["g_emb"]),
    )
    groups = [(way(a), way(b), way(c), g) for way, a, b, c, g in plan]
    results = run_update(items_all, step_count, grads["totals"], groups)
    updated = [plan[k // 3][0](results[k]) for k in range(21)]
    loss, norm, rms = results[21:]
    return (loss.reshape(()), norm.reshape(()), *updated, rms[2:6, 0])


def solution(mesh):
    return jax.shard_map(
        body,
        mesh=mesh,
        in_specs=(
            P("dp", "var", None, None),
            P("dp", None, None),
            P("dp"),
            P(),
            P("var"),
            P(),
            P(None, "dp", ("var", "mp")),
            P(None, "dp", ("var", "mp")),
            P(None, "dp", ("var", "mp")),
            P(None, "dp", ("var", "mp")),
            P(None, "dp", ("var", "mp")),
            P(None, "dp", ("var", "mp")),
            P(None, ("dp", "var"), "mp"),
            P(None, ("dp", "var"), "mp"),
            P(None, ("dp", "var"), "mp"),
            P(None, ("dp", "var", "mp")),
            P(None, ("dp", "var", "mp")),
            P(None, ("dp", "var", "mp")),
            P(None, ("dp", "var", "mp")),
            P(None, ("dp", "var", "mp")),
            P(None, ("dp", "var", "mp")),
            P(None, ("dp", "var", "mp")),
            P(None, ("dp", "var", "mp")),
            P(None, ("dp", "var", "mp")),
            P(None, ("dp", "var", "mp")),
            P(None, ("dp", "var", "mp")),
            P(None, ("dp", "var", "mp")),
        ),
        out_specs=(
            P(),
            P(),
            P(None, "dp", ("var", "mp")),
            P(None, "dp", ("var", "mp")),
            P(None, "dp", ("var", "mp")),
            P(None, "dp", ("var", "mp")),
            P(None, "dp", ("var", "mp")),
            P(None, "dp", ("var", "mp")),
            P(None, ("dp", "var"), "mp"),
            P(None, ("dp", "var"), "mp"),
            P(None, ("dp", "var"), "mp"),
            P(None, ("dp", "var", "mp")),
            P(None, ("dp", "var", "mp")),
            P(None, ("dp", "var", "mp")),
            P(None, ("dp", "var", "mp")),
            P(None, ("dp", "var", "mp")),
            P(None, ("dp", "var", "mp")),
            P(None, ("dp", "var", "mp")),
            P(None, ("dp", "var", "mp")),
            P(None, ("dp", "var", "mp")),
            P(None, ("dp", "var", "mp")),
            P(None, ("dp", "var", "mp")),
            P(None, ("dp", "var", "mp")),
            P(),
        ),
        check_vma=False,
    )
```
